128 devices in a mesh: seq: 32 (over y, x, core), head: 4 (over z).
Axes of the slice: x: 4, y: 4, z: 4, core: 2. Of those that a mesh axis runs over, the one named last changes fastest.
Arguments:
- queries: bfloat16 [131072, 1024], P('seq', 'head'), may hold values from -720 to 720
- keys: bfloat16 [131072, 1024], P('seq', 'head'), may hold values from -6 to 6
- values: bfloat16 [131072, 1024], P('seq', 'head'), may hold values from -6 to 6
- cluster: int32 [1024, 1], P('seq'), may hold values from 0 to 31; in each aligned block of 32 rows (0 to 31, 32 to 63, ...) at most 2 rows name the same one
- w_out: bfloat16 [1024, 1024], P('head'), may hold values from -0.5 to 0.5
Outputs:
- mixed: bfloat16 [131072, 1024], P('seq', 'head')
The draws below stay inside these ranges and needn't reach their ends.
Inputs may be any that keep to these rules, and one draw needn't show every extreme that they name: In the 32 blocks of one index of seq no cluster is named more than 2 times, and on some index of seq a cluster is named exactly 2 times.
All inputs are finite; a program needn't handle non-finite values.
Results may differ from the reference program's by a relative error of at most 0.0054.
Values may be sent and summed in bfloat16 or wider, within the bound.
A program may use at most 128 MiB of HBM per device.

```python
import math
import jax
import jax.numpy as jnp
import numpy as np
from jax import lax

HEADS = 16
HEAD_DIM = 64
BLOCK = 128
BLK_DEV = 32
D = 1024
TOKENS = 131072
NBLK = 1024
NCLUST = 32
MOST = 2
N_SEQ = 32


def draw_pair(key):
    base_keys = jnp.clip(jax.random.normal(jax.random.fold_in(key, 101), (TOKENS, D), jnp.float32), -6.0, 6.0)
    base_queries = jnp.clip(jax.random.normal(jax.random.fold_in(key, 202), (TOKENS, D), jnp.float32), -6.0, 6.0)
    return (base_queries, base_keys)


def draw_queries(key, part):
    return draw_pair(key)[0].astype(jnp.bfloat16)


def draw_keys(key, part):
    return draw_pair(key)[1].astype(jnp.bfloat16)


def levels(key, shape, pieces, low, largest):
    level, own = 1.0, jax.random.fold_in(key, 6)
    for dim, blocks in pieces:
        steps = jnp.exp(jax.random.uniform(jax.random.fold_in(own, dim), (blocks,), jnp.float32, low / len(pieces), largest / len(pieces)))
        level = level * jnp.repeat(steps, shape[dim] // blocks).reshape([-1 if axis == dim else 1 for axis in range(len(shape))])
    return level


def assign_block(rng, own, number, rows, amount, top, limit, skew):
    ranking = jax.random.permutation(rng, amount)
    crowded, ordinary = portions_of(amount, rows * top, limit, skew, True), portions_of(amount, rows * top, limit, skew, False)
    places = jnp.arange(amount)

    def named(tallies, turn):
        used = int((tallies > 0).sum())
        fixed = max(1, used // 4)
        shifted = fixed + (places - fixed + turn * (used - fixed)) % max(1, amount - fixed)
        return jnp.zeros((amount,), jnp.int32).at[ranking[jnp.where(places < fixed, places, shifted)]].set(jnp.asarray(tallies, jnp.int32))

    tallies = jnp.where(number % 4 == 0, named(crowded, number // 4), named(ordinary, number - number // 4 - 1))
    mixed = jax.random.permutation(jax.random.fold_in(own, 3), amount)
    giver, sink = mixed[0:amount // 2 * 2:2], mixed[1:amount // 2 * 2:2]
    room = jnp.minimum(tallies[giver] - 1, limit - tallies[sink]) // 2
    room = jnp.where((giver == ranking[0]) | (sink == ranking[0]) | (tallies[sink] == 0), 0, jnp.maximum(room, 0))
    shifted = jax.random.randint(jax.random.fold_in(own, 4), (amount // 2,), 0, 1 << 20) % (room + 1)
    tallies = tallies.at[giver].add(-shifted).at[sink].add(shifted)
    members = jnp.searchsorted(jnp.cumsum(tallies), jnp.arange(rows * top), side="right").astype(jnp.int32)
    listing = members.reshape(top, rows).T
    listing = listing[jax.random.permutation(jax.random.fold_in(own, 1), rows)]
    turn = jax.random.randint(jax.random.fold_in(own, 2), (rows, 1), 0, top)
    return jnp.take_along_axis(listing, (jnp.arange(top)[None, :] + turn) % top, axis=1)


def portions_of(number_of, total, most, slope, full):
    weights = [(1 << 20) // math.isqrt(rank ** slope) + 1 for rank in range(1, number_of + 1)]
    largest = most if full else min(most, max(-(-total // number_of), total * weights[0] // sum(weights)))
    least = 1 if total - largest >= number_of - 1 else 0
    holding, spare = [largest] + [least] * (number_of - 1), total - largest - least * (number_of - 1)
    while spare > 0:
        free = [i for i in range(1, number_of) if holding[i] < largest] or [i for i in range(1, number_of) if holding[i] < most]
        pool, left = sum([weights[i] for i in free]), spare
        for i in free:
            extra = min(most - holding[i], max(1, left * weights[i] // pool), spare)
            holding[i] = holding[i] + extra
            spare = spare - extra
    return np.array(holding)


def scatter_about(key, dims, width, reach, split=(), kind=jnp.bfloat16):
    factor_of = levels(key, dims, split, -0.22, 0.18) if split else 1.0
    result = jax.random.normal(key, dims, jnp.float32) * width * factor_of
    return jnp.minimum(jnp.maximum(result, -reach), reach).astype(kind)


def setup_inputs(seed: int = 0) -> dict:
    seeds = jax.random.split(jax.random.key(seed), 6)
    queries = draw_queries(jax.random.fold_in(seeds[5], 71), 0)
    keys = draw_keys(jax.random.fold_in(seeds[5], 71), 0)
    values = scatter_about(seeds[2], (TOKENS, D), 1.0, 6.0, ((0, 32), (1, 4)))
    cluster_keys = jax.random.split(jax.random.fold_in(seeds[3], 1), NBLK // BLK_DEV)
    cluster_turns = jax.random.permutation(jax.random.fold_in(seeds[3], 3), NBLK // BLK_DEV)
    cluster = jax.vmap(lambda own, number: assign_block(jax.random.fold_in(seeds[3], 2), own, number, BLK_DEV, NCLUST, 1, MOST, 1))(cluster_keys, cluster_turns).reshape((NBLK, 1))
    w_out = scatter_about(seeds[4], (D, D), (2 * HEAD_DIM) ** -0.5, 0.5, ((0, 4),))
    return dict(queries=queries, keys=keys, values=values, cluster=cluster, w_out=w_out)


def reference(queries, keys, values, cluster, w_out):
    block_total = cluster.shape[0]
    cluster_list = cluster[:, 0].astype(jnp.int32)
    capacity = N_SEQ * MOST
    score_scale = HEAD_DIM ** -0.5
    sorted_order = jnp.argsort(cluster_list * block_total + jnp.arange(block_total, dtype=jnp.int32)).astype(jnp.int32)
    sorted_clusters = cluster_list[sorted_order]
    cluster_range = jnp.arange(NCLUST, dtype=jnp.int32)
    cluster_start = jnp.sum((cluster_list[None, :] < cluster_range[:, None]).astype(jnp.int32), axis=1).astype(jnp.int32)
    order_padded = jnp.concatenate([sorted_order, jnp.zeros((capacity,), jnp.int32)])
    clusters_padded = jnp.concatenate([sorted_clusters, jnp.full((capacity,), -1, jnp.int32)])
    query_blocks = queries.reshape(block_total, BLOCK, HEADS, HEAD_DIM)
    key_blocks_all = keys.reshape(block_total, BLOCK, HEADS, HEAD_DIM)
    value_blocks_all = values.reshape(block_total, BLOCK, HEADS, HEAD_DIM)
    row_offset = jnp.arange(BLOCK, dtype=jnp.int32)
    key_offset = jnp.tile(row_offset, capacity)

    def attend_block(block_index):
        cluster_now = cluster_list[block_index]
        start_at = cluster_start[cluster_now]
        key_blocks = lax.dynamic_slice(order_padded, (start_at,), (capacity,))
        key_clusters = lax.dynamic_slice(clusters_padded, (start_at,), (capacity,))
        key_allowed = (key_clusters == cluster_now) & (key_blocks <= block_index)
        key_rows = key_blocks_all[key_blocks].reshape(capacity * BLOCK, HEADS, HEAD_DIM).astype(jnp.float32)
        value_rows = value_blocks_all[key_blocks].reshape(capacity * BLOCK, HEADS, HEAD_DIM).astype(jnp.float32)
        query_rows = query_blocks[block_index].astype(jnp.float32)
        scores = jnp.einsum("qhd,khd->hqk", query_rows, key_rows) * score_scale
        key_block_rows = jnp.repeat(key_blocks, BLOCK)
        key_live = jnp.repeat(key_allowed, BLOCK)
        permitted = key_live[None, :] & ((key_block_rows[None, :] < block_index) | (key_offset[None, :] <= row_offset[:, None]))
        scores = jnp.where(permitted[None], scores, jnp.float32(-1e30))
        row_max = jnp.max(scores, axis=2)
        weights = jnp.exp(scores - row_max[:, :, None])
        weight_sum = jnp.sum(weights, axis=2)
        rounded = lax.optimization_barrier(weights.astype(jnp.bfloat16)).astype(jnp.float32)
        output = jnp.einsum("hqk,khd->qhd", rounded, value_rows) / weight_sum.T[:, :, None]
        return output.astype(jnp.bfloat16).reshape(BLOCK, HEADS * HEAD_DIM)

    attended = lax.map(attend_block, jnp.arange(block_total, dtype=jnp.int32)).reshape(TOKENS, D)
    return jnp.dot(attended, w_out, preferred_element_type=jnp.float32).astype(jnp.bfloat16)
```

```python
import functools

import jax
import jax.numpy as jnp
from jax import lax
from jax.experimental import pallas as pl
from jax.experimental.pallas import tpu as pltpu
from jax.sharding import PartitionSpec as P

HEADS = 16
BLOCK = 128
HEAD = 64
MAIN = 5
FULL = 8
TILE = 4
NT = (((1,), (1,)), ((), ()))


def tables(cluster):
    n = lax.axis_size("seq")
    me = lax.axis_index("seq")
    blocks = cluster.shape[0]
    mine = cluster.reshape(blocks)
    everyone = lax.all_to_all(
        jnp.broadcast_to(mine[None, :], (n, blocks)), "seq", split_axis=0, concat_axis=0, tiled=True
    )
    ids = jnp.arange(n, dtype=jnp.int32)
    heads = jnp.arange(4, dtype=jnp.int32)
    counts = jnp.sum((everyone[:, :, None] == ids).astype(jnp.int32), axis=1)
    weight = jnp.max(counts, axis=0)
    before = ids[None, :] < ids[:, None]
    rank2 = jnp.sum((before & (weight == 2)[None, :]).astype(jnp.int32), axis=1)
    rank1 = jnp.sum((before & (weight == 1)[None, :]).astype(jnp.int32), axis=1)
    twos = 4 * jnp.sum((weight == 2).astype(jnp.int32))
    full, rem = twos // n, twos % n
    light = n - rem
    heavy = jnp.maximum(rem, 1)
    k2 = rank2[:, None] * 4 + heads
    k = rank1[:, None] * 4 + heads
    a = jnp.maximum(MAIN - 2 * full, 0) * light
    b = jnp.maximum(MAIN - 2 - 2 * full, 0) * rem
    c0 = jnp.maximum(MAIN, 2 * full)
    c = (FULL - c0) * light
    kb, kc = k - a, k - a - b
    kd = kc - c
    owner1 = jnp.where(
        k < a, rem + k % light, jnp.where(kb < b, kb % heavy, jnp.where(kc < c, rem + kc % light, kd % heavy))
    )
    slot1 = jnp.where(
        k < a,
        2 * full + k // light,
        jnp.where(
            kb < b,
            2 * full + 2 + kb // heavy,
            jnp.where(kc < c, c0 + kc // light, jnp.maximum(MAIN, 2 * full + 2) + kd // heavy),
        ),
    )
    two = (weight == 2)[:, None]
    used = (weight > 0)[:, None]
    owner = jnp.where(two, k2 % n, owner1)
    slot = jnp.where(two, 2 * (k2 // n), slot1)
    fits = jnp.all(~used | (slot + weight[:, None] <= MAIN))
    hit = mine[:, None] == ids[None, :]
    earlier = jnp.arange(blocks)[None, :] < jnp.arange(blocks)[:, None]
    second = jnp.sum((earlier & (mine[None, :] == mine[:, None])).astype(jnp.int32), axis=1)
    target = jnp.sum(jnp.where(hit[:, :, None], (owner * FULL + slot)[None], 0), axis=1) + second[:, None]
    slots = jnp.arange(FULL, dtype=jnp.int32)
    held = (used & (owner == me))[None] & (slot[None] == slots[:, None, None])
    unit = jnp.sum(jnp.where(held, weight[None, :, None], 0), axis=(1, 2))
    count = jnp.sum(jnp.where(jnp.any(held, axis=2)[:, None, :], counts[None], 0), axis=2)
    return fits, target.reshape(blocks * 4), unit, count.reshape(FULL * n)


PACK = 4


def pack_kernel(target, q_ref, k_ref, v_ref, out_ref, stage, eye, sems):
    step = pl.program_id(0)
    par = lax.rem(step, 2)

    @pl.when(step == 0)
    def _():
        r = lax.broadcasted_iota(jnp.int32, (256, 256), 0)
        c = lax.broadcasted_iota(jnp.int32, (256, 256), 1)
        eye[...] = jnp.where(r == c, 1.0, 0.0).astype(jnp.bfloat16)

    def copy(at, p, i):
        t = target[at * (PACK * 4) + i]
        return pltpu.make_async_copy(
            stage.at[p, i], out_ref.at[lax.div(t, FULL), lax.rem(t, FULL)], sems.at[p, i]
        )

    @pl.when(step >= 2)
    def _():
        for i in range(PACK * 4):
            copy(step - 2, par, i).wait()

    lane = lax.broadcasted_iota(jnp.int32, (BLOCK, 128), 1)
    for t in range(PACK):
        rows = slice(t * BLOCK, (t + 1) * BLOCK)
        vt = lax.dot_general(eye[...], v_ref[rows, :], NT, preferred_element_type=jnp.float32)
        vt = vt.astype(jnp.bfloat16)
        for pair in range(2):
            cols = slice(pair * 128, (pair + 1) * 128)
            q = q_ref[rows, cols].astype(jnp.float32)
            k = k_ref[rows, cols].astype(jnp.float32)
            even = jnp.where(lane < HEAD, q, pltpu.roll(k, HEAD, 1))
            odd = jnp.where(lane < HEAD, pltpu.roll(q, HEAD, 1), k)
            stage[par, t * 4 + pair * 2, 0:BLOCK, :] = even.astype(jnp.bfloat16)
            stage[par, t * 4 + pair * 2 + 1, 0:BLOCK, :] = odd.astype(jnp.bfloat16)
        for h in range(4):
            stage[par, t * 4 + h, BLOCK : BLOCK + HEAD, :] = vt[h * HEAD : (h + 1) * HEAD]
    for i in range(PACK * 4):
        copy(step, par, i).start()

    @pl.when(step == pl.num_programs(0) - 1)
    def _():
        for i in range(PACK * 4):
            copy(step - 1, 1 - par, i).wait()
        for i in range(PACK * 4):
            copy(step, par, i).wait()


def pack(target, queries, keys, values, n, depth):
    rows, width = queries.shape
    tile = pl.BlockSpec((PACK * BLOCK, width), lambda i, *_: (i, 0))
    return pl.pallas_call(
        pack_kernel,
        out_shape=jax.ShapeDtypeStruct((n, depth, BLOCK + HEAD, 128), jnp.bfloat16),
        grid_spec=pltpu.PrefetchScalarGridSpec(
            num_scalar_prefetch=1,
            grid=(rows // (PACK * BLOCK),),
            in_specs=[tile, tile, tile],
            out_specs=pl.BlockSpec(memory_space=pl.ANY),
            scratch_shapes=[
                pltpu.VMEM((2, PACK * 4, BLOCK + HEAD, 128), jnp.bfloat16),
                pltpu.VMEM((256, 256), jnp.bfloat16),
                pltpu.SemaphoreType.DMA((2, PACK * 4)),
            ],
        ),
        name=f"pack{depth}",
    )(target, queries, keys, values)


def attend_kernel(depth, n, unit, count, recv, out, kq, vt, stage, where_from, sizes, pending, in_sems, out_sems):
    tq = TILE * BLOCK

    def fetch(pos, s, j, u):
        at = pl.multiple_of(pos * BLOCK, BLOCK)
        return (
            pltpu.make_async_copy(
                recv.at[s, j, pl.ds(0, BLOCK), :], kq.at[pl.ds(at, BLOCK), :], in_sems.at[u, 0]
            ),
            pltpu.make_async_copy(
                recv.at[s, j, pl.ds(BLOCK, HEAD), :],
                vt.at[pl.ds(0, HEAD), pl.ds(at, BLOCK)],
                in_sems.at[u, 1],
            ),
        )

    def fetch_unit(u, base):
        w = unit[u]

        def source(s, pos):
            here = jnp.where(w > 0, count[u * n + s], 0)
            for r in range(2):

                @pl.when(here > r)
                def _():
                    where_from[pos + r] = s * depth + u + r
                    for c in fetch(pos + r, s, u + r, u):
                        c.start()

            return pos + here

        end = lax.fori_loop(0, n, source, base)
        sizes[u] = end - base
        stop = lax.div(end + TILE - 1, TILE) * TILE

        def blank(pos, c):
            at = pl.multiple_of(pos * BLOCK, BLOCK)
            vt[0:HEAD, pl.ds(at, BLOCK)] = jnp.zeros((HEAD, BLOCK), jnp.bfloat16)
            return c

        lax.fori_loop(end, stop, blank, 0)
        return stop

    lax.fori_loop(0, depth, fetch_unit, 0)
    ones = lax.broadcasted_iota(jnp.int32, (16, vt.shape[1]), 0)
    vt[HEAD : HEAD + 16, :] = jnp.where(ones == 0, 1.0, 0.0).astype(jnp.bfloat16)
    for p in range(2):
        for t in range(TILE):
            pending[p * TILE + t] = 0

    lane = lax.broadcasted_iota(jnp.int32, (tq, 128), 1)
    krow = lax.broadcasted_iota(jnp.int32, (tq, tq), 0)
    qcol = lax.broadcasted_iota(jnp.int32, (tq, tq), 1)
    er = lax.broadcasted_iota(jnp.int32, (BLOCK, BLOCK), 0)
    ec = lax.broadcasted_iota(jnp.int32, (BLOCK, BLOCK), 1)
    eye = jnp.where(er == ec, 1.0, 0.0).astype(jnp.bfloat16)
    low = ec < HEAD

    def put(p, t, pos):
        f = where_from[pos]
        return pltpu.make_async_copy(
            stage.at[p, t],
            out.at[pl.ds(lax.div(f, depth) * 4, 4), lax.rem(f, depth)],
            out_sems.at[p, t],
        )

    def run_unit(u, carry):
        base, turn = carry
        size = sizes[u]

        def arrive(i, c):
            for cp in fetch(0, 0, 0, u):
                cp.wait()
            return c

        lax.fori_loop(0, size, arrive, 0)

        def q_tile(i, turn):
            q0 = pl.multiple_of((base + i * TILE) * BLOCK, tq)
            x = kq[pl.ds(q0, tq), :].astype(jnp.float32)
            q = jnp.where(lane >= HEAD, pltpu.roll(x, HEAD, 1) * 0.125, 0.0).astype(jnp.bfloat16)

            def k_tile(at, top, acc, masked):
                at = pl.multiple_of(at, tq)
                s = lax.dot_general(kq[pl.ds(at, tq), :], q, NT, preferred_element_type=jnp.float32)
                if masked:
                    s = jnp.where(krow <= qcol, s, -1e30)
                newer = jnp.maximum(top, jnp.max(s, axis=0, keepdims=True))
                weights = jnp.exp(s - newer).astype(jnp.bfloat16)
                part = jnp.dot(vt[:, pl.ds(at, tq)], weights, preferred_element_type=jnp.float32)
                return newer, acc * jnp.exp(top - newer) + part

            def step(j, c):
                return k_tile((base + j * TILE) * BLOCK, c[0], c[1], False)

            top, acc = lax.fori_loop(
                0,
                i,
                step,
                (jnp.full((1, tq), -1e30, jnp.float32), jnp.zeros((HEAD + 16, tq), jnp.float32)),
            )
            top, acc = k_tile(q0, top, acc, True)
            o = (acc[0:HEAD] / acc[HEAD : HEAD + 1]).astype(jnp.bfloat16)
            p = lax.rem(turn, 2)
            for t in range(TILE):
                pos = base + i * TILE + t

                @pl.when(pending[p * TILE + t] == 1)
                def _():
                    put(p, t, base).wait()

                piece = o[:, t * BLOCK : (t + 1) * BLOCK]
                both = jnp.concatenate([piece, piece], axis=0)
                flat = lax.dot_general(eye, both, NT, preferred_element_type=jnp.float32)
                packed = jnp.where(low[0:HEAD], flat[0:HEAD], flat[HEAD:BLOCK]).astype(jnp.bfloat16)
                stage[p, t] = packed.reshape(4, 16, 128)
                live = i * TILE + t < size
                pending[p * TILE + t] = live.astype(jnp.int32)

                @pl.when(live)
                def _():
                    put(p, t, pos).start()

            return turn + 1

        tiles = lax.div(size + TILE - 1, TILE)
        turn = lax.fori_loop(0, tiles, q_tile, turn)
        return base + tiles * TILE, turn

    lax.fori_loop(0, depth, run_unit, (0, 0))
    for p in range(2):
        for t in range(TILE):

            @pl.when(pending[p * TILE + t] == 1)
            def _():
                put(p, t, 0).wait()


def attend(unit, count, recv):
    n, depth = recv.shape[:2]
    room = depth * n + depth * (TILE - 1)
    room = -(-room // TILE) * TILE
    smem = pl.BlockSpec(memory_space=pltpu.SMEM)
    return pl.pallas_call(
        functools.partial(attend_kernel, depth, n),
        out_shape=jax.ShapeDtypeStruct((n * 4, depth, 16, 128), jnp.bfloat16),
        in_specs=[smem, smem, pl.BlockSpec(memory_space=pl.ANY)],
        out_specs=pl.BlockSpec(memory_space=pl.ANY),
        scratch_shapes=[
            pltpu.VMEM((room * BLOCK, 128), jnp.bfloat16),
            pltpu.VMEM((HEAD + 16, room * BLOCK), jnp.bfloat16),
            pltpu.VMEM((2, TILE, 4, 16, 128), jnp.bfloat16),
            pltpu.SMEM((room + 4,), jnp.int32),
            pltpu.SMEM((depth,), jnp.int32),
            pltpu.SMEM((2 * TILE,), jnp.int32),
            pltpu.SemaphoreType.DMA((depth, 2)),
            pltpu.SemaphoreType.DMA((2, TILE)),
        ],
        compiler_params=pltpu.CompilerParams(vmem_limit_bytes=60 * 2**20),
        name=f"attend{depth}",
    )(unit, count, recv)


PROJ = 8


def project_kernel(target, got, w_ref, out_ref, att):
    step = pl.program_id(0)
    lane = lax.broadcasted_iota(jnp.int32, (16, 128), 1)
    for t in range(PROJ):
        for pair in range(2):
            at = (step * PROJ + t) * 4 + pair * 2
            ea, eb = target[at], target[at + 1]
            for z in range(4):
                even = got[lax.div(ea, FULL) * 4 + z, lax.rem(ea, FULL)].astype(jnp.float32)
                odd = got[lax.div(eb, FULL) * 4 + z, lax.rem(eb, FULL)].astype(jnp.float32)
                cols = slice(z * 256 + pair * 128, z * 256 + pair * 128 + 128)
                lo = jnp.where(lane < HEAD, even, pltpu.roll(odd, HEAD, 1))
                hi = jnp.where(lane < HEAD, pltpu.roll(even, HEAD, 1), odd)
                att[t * 32 : t * 32 + 16, cols] = lo.astype(jnp.bfloat16)
                att[t * 32 + 16 : t * 32 + 32, cols] = hi.astype(jnp.bfloat16)
    mixed = jnp.zeros((PROJ * 32, 1024), jnp.float32)
    for z in range(4):
        mixed += jnp.dot(att[:, z * 256 : (z + 1) * 256], w_ref[z], preferred_element_type=jnp.float32)
    mixed = mixed.astype(jnp.bfloat16)
    for z in range(4):
        out_ref[z] = mixed[:, z * 256 : (z + 1) * 256].reshape(PROJ, 2, 16, 256)


def project(target, got, w_full, blocks):
    return pl.pallas_call(
        project_kernel,
        out_shape=jax.ShapeDtypeStruct((4, blocks, 2, 16, 256), jnp.bfloat16),
        grid_spec=pltpu.PrefetchScalarGridSpec(
            num_scalar_prefetch=1,
            grid=(blocks // PROJ,),
            in_specs=[
                pl.BlockSpec(got.shape, lambda i, *_: (0, 0, 0, 0)),
                pl.BlockSpec(w_full.shape, lambda i, *_: (0, 0, 0)),
            ],
            out_specs=pl.BlockSpec((4, PROJ, 2, 16, 256), lambda i, *_: (0, i, 0, 0, 0)),
            scratch_shapes=[pltpu.VMEM((PROJ * 32, 1024), jnp.bfloat16)],
        ),
        name=f"project{got.shape[1]}",
    )(target, got, w_full)


def route(depth, target, unit, count, queries, keys, values, w_full):
    n = lax.axis_size("seq")
    blocks = queries.shape[0] // BLOCK
    sent = pack(target, queries, keys, values, n, depth)
    recv = lax.all_to_all(sent, "seq", split_axis=0, concat_axis=0, tiled=True)
    answers = attend(unit, count, recv)
    got = lax.all_to_all(answers, ("seq", "head"), split_axis=0, concat_axis=0, tiled=True)
    mixed = project(target, got, w_full, blocks)
    back = lax.all_to_all(mixed, "head", split_axis=0, concat_axis=0, tiled=True)
    return back.transpose(1, 2, 0, 3, 4).reshape(queries.shape)


def body(queries, keys, values, cluster, w_out):
    fits, target, unit, count = tables(cluster)
    w_full = lax.all_to_all(
        jnp.broadcast_to(w_out[None], (4,) + w_out.shape), "head", split_axis=0, concat_axis=0, tiled=True
    )
    return lax.cond(
        fits,
        functools.partial(route, MAIN),
        functools.partial(route, FULL),
        target,
        unit,
        count,
        queries,
        keys,
        values,
        w_full,
    )


def solution(mesh):
    placed = (P("seq", "head"), P("seq", "head"), P("seq", "head"), P("seq", None), P("head", None))
    return jax.shard_map(
        body, mesh=mesh, in_specs=placed, out_specs=P("seq", "head"), check_vma=False
    )
```

```python
import functools

import jax
import jax.numpy as jnp
from jax import lax
from jax.experimental import pallas as pl
from jax.experimental.pallas import tpu as pltpu
from jax.sharding import PartitionSpec as P


BLOCK = 128
HEAD = 64
MAIN = 5
FIRST = 2
FULL = 8
TILE = 4
NT = (((1,), (1,)), ((), ()))


def tables(cluster):
    n = lax.axis_size("seq")
    me = lax.axis_index("seq")
    blocks = cluster.shape[0]
    mine = cluster.reshape(blocks)
    everyone = lax.all_to_all(
        jnp.broadcast_to(mine[None, :], (n, blocks)), "seq", split_axis=0, concat_axis=0, tiled=True
    )
    ids = jnp.arange(n, dtype=jnp.int32)
    heads = jnp.arange(4, dtype=jnp.int32)
    counts = jnp.sum((everyone[:, :, None] == ids).astype(jnp.int32), axis=1)
    weight = jnp.max(counts, axis=0)
    before = ids[None, :] < ids[:, None]
    rank2 = jnp.sum((before & (weight == 2)[None, :]).astype(jnp.int32), axis=1)
    rank1 = jnp.sum((before & (weight == 1)[None, :]).astype(jnp.int32), axis=1)
    twos = 4 * jnp.sum((weight == 2).astype(jnp.int32))
    full, rem = twos // n, twos % n
    light = n - rem
    heavy = jnp.maximum(rem, 1)
    k2 = rank2[:, None] * 4 + heads
    k = rank1[:, None] * 4 + heads
    a = jnp.maximum(MAIN - 2 * full, 0) * light
    b = jnp.maximum(MAIN - 2 - 2 * full, 0) * rem
    c0 = jnp.maximum(MAIN, 2 * full)
    c = (FULL - c0) * light
    kb, kc = k - a, k - a - b
    kd = kc - c
    owner1 = jnp.where(
        k < a, rem + k % light, jnp.where(kb < b, kb % heavy, jnp.where(kc < c, rem + kc % light, kd % heavy))
    )
    slot1 = jnp.where(
        k < a,
        2 * full + k // light,
        jnp.where(
            kb < b,
            2 * full + 2 + kb // heavy,
            jnp.where(kc < c, c0 + kc // light, jnp.maximum(MAIN, 2 * full + 2) + kd // heavy),
        ),
    )
    two = (weight == 2)[:, None]
    used = (weight > 0)[:, None]
    owner = jnp.where(two, k2 % n, owner1)
    slot = jnp.where(two, 2 * (k2 // n), slot1)
    fits = jnp.all(~used | (slot + weight[:, None] <= MAIN))
    hit = mine[:, None] == ids[None, :]
    earlier = jnp.arange(blocks)[None, :] < jnp.arange(blocks)[:, None]
    second = jnp.sum((earlier & (mine[None, :] == mine[:, None])).astype(jnp.int32), axis=1)
    target = jnp.sum(jnp.where(hit[:, :, None], (owner * FULL + slot)[None], 0), axis=1) + second[:, None]
    slots = jnp.arange(FULL, dtype=jnp.int32)
    held = (used & (owner == me))[None] & (slot[None] == slots[:, None, None])
    unit = jnp.sum(jnp.where(held, weight[None, :, None], 0), axis=(1, 2))
    count = jnp.sum(jnp.where(jnp.any(held, axis=2)[:, None, :], counts[None], 0), axis=2)
    return fits, target.reshape(blocks * 4), unit, count.reshape(FULL * n)


PACK = 4


def pack_kernel(target, q_ref, k_ref, v_ref, one_ref, two_ref, stage, eye, sems):
    step = pl.program_id(0)
    par = lax.rem(step, 2)

    @pl.when(step == 0)
    def _():
        r = lax.broadcasted_iota(jnp.int32, (256, 256), 0)
        c = lax.broadcasted_iota(jnp.int32, (256, 256), 1)
        eye[...] = jnp.where(r == c, 1.0, 0.0).astype(jnp.bfloat16)

    def send(p, i):
        t = target[step * (PACK * 4) + i]
        owner, slot = lax.div(t, FULL), lax.rem(t, FULL)

        @pl.when(slot < FIRST)
        def _():
            pltpu.make_async_copy(stage.at[p, i], one_ref.at[owner, slot], sems.at[p, i]).start()

        @pl.when(slot >= FIRST)
        def _():
            pltpu.make_async_copy(stage.at[p, i], two_ref.at[owner, slot - FIRST], sems.at[p, i]).start()

    def wait(p, i):
        pltpu.make_async_copy(stage.at[p, i], one_ref.at[0, 0], sems.at[p, i]).wait()

    @pl.when(step >= 2)
    def _():
        for i in range(PACK * 4):
            wait(par, i)

    lane = lax.broadcasted_iota(jnp.int32, (BLOCK, 128), 1)
    for t in range(PACK):
        rows = slice(t * BLOCK, (t + 1) * BLOCK)
        vt = lax.dot_general(eye[...], v_ref[rows, :], NT, preferred_element_type=jnp.float32)
        vt = vt.astype(jnp.bfloat16)
        for pair in range(2):
            cols = slice(pair * 128, (pair + 1) * 128)
            q = q_ref[rows, cols].astype(jnp.float32)
            k = k_ref[rows, cols].astype(jnp.float32)
            even = jnp.where(lane < HEAD, q, pltpu.roll(k, HEAD, 1))
            odd = jnp.where(lane < HEAD, pltpu.roll(q, HEAD, 1), k)
            stage[par, t * 4 + pair * 2, 0:BLOCK, :] = even.astype(jnp.bfloat16)
            stage[par, t * 4 + pair * 2 + 1, 0:BLOCK, :] = odd.astype(jnp.bfloat16)
        for h in range(4):
            stage[par, t * 4 + h, BLOCK : BLOCK + HEAD, :] = vt[h * HEAD : (h + 1) * HEAD]
    for i in range(PACK * 4):
        send(par, i)

    @pl.when(step == pl.num_programs(0) - 1)
    def _():
        for i in range(PACK * 4):
            wait(1 - par, i)
        for i in range(PACK * 4):
            wait(par, i)


def pack(target, queries, keys, values, n, depth):
    rows, width = queries.shape
    tile = pl.BlockSpec((PACK * BLOCK, width), lambda i, *_: (i, 0))
    return pl.pallas_call(
        pack_kernel,
        out_shape=[
            jax.ShapeDtypeStruct((n, d, BLOCK + HEAD, 128), jnp.bfloat16) for d in (FIRST, depth - FIRST)
        ],
        grid_spec=pltpu.PrefetchScalarGridSpec(
            num_scalar_prefetch=1,
            grid=(rows // (PACK * BLOCK),),
            in_specs=[tile, tile, tile],
            out_specs=[pl.BlockSpec(memory_space=pl.ANY)] * 2,
            scratch_shapes=[
                pltpu.VMEM((2, PACK * 4, BLOCK + HEAD, 128), jnp.bfloat16),
                pltpu.VMEM((256, 256), jnp.bfloat16),
                pltpu.SemaphoreType.DMA((2, PACK * 4)),
            ],
        ),
    )(target, queries, keys, values)


def attend_kernel(
    depth, offset, n, unit, count, recv, _, out, kq, qz, vt, score0, score1, top, acc, flat, where_from, steps, in_sems, out_sem
):
    tq = TILE * BLOCK
    spare = acc.shape[0] - 1

    def fetch(pos, s, j, u):
        at = pl.multiple_of(pos * BLOCK, BLOCK)
        return (
            pltpu.make_async_copy(
                recv.at[s, j, pl.ds(0, BLOCK), :], kq.at[pl.ds(at, BLOCK), :], in_sems.at[u, 0]
            ),
            pltpu.make_async_copy(
                recv.at[s, j, pl.ds(BLOCK, HEAD), :],
                vt.at[pl.ds(0, HEAD), pl.ds(at, BLOCK)],
                in_sems.at[u, 1],
            ),
        )

    def fetch_unit(u, carry):
        base, listed, total = carry
        w = unit[u]

        def source(s, pos):
            here = jnp.where(w > 0, count[u * n + s], 0)
            for r in range(2):

                @pl.when(here > r)
                def _():
                    where_from[pos + r] = s * depth + u + r
                    for c in fetch(pos + r, s, u + r, u):
                        c.start()

            return pos + here

        end = lax.fori_loop(0, n, source, base)
        stop = lax.div(end + TILE - 1, TILE) * TILE

        def blank(pos, c):
            at = pl.multiple_of(pos * BLOCK, BLOCK)
            vt[0:HEAD, pl.ds(at, BLOCK)] = jnp.zeros((HEAD, BLOCK), jnp.bfloat16)
            where_from[pos] = -1
            return c

        lax.fori_loop(end, stop, blank, 0)
        first, last = lax.div(base, TILE), lax.div(stop, TILE)

        def list_tile(q, at):
            def one(k, at):
                steps[at] = q * 256 + k
                return at + 1

            return lax.fori_loop(first, q, one, at)

        return stop, lax.fori_loop(first, last, list_tile, listed), total + end - base

    stop, listed, total = lax.fori_loop(0, depth, fetch_unit, (0, 0, 0))
    tiles = lax.div(stop, TILE)
    for extra in range(3):
        steps[listed + extra] = spare * 256 + spare
    ones = lax.broadcasted_iota(jnp.int32, (16, vt.shape[1]), 0)
    vt[HEAD : HEAD + 16, :] = jnp.where(ones == 0, 1.0, 0.0).astype(jnp.bfloat16)

    def arrive(u, c):
        def one(s, c):
            here = jnp.where(unit[u] > 0, count[u * n + s], 0)
            for r in range(2):

                @pl.when(here > r)
                def _():
                    for cp in fetch(0, 0, 0, u):
                        cp.wait()

            return c

        return lax.fori_loop(0, n, one, c)

    lax.fori_loop(0, depth, arrive, 0)

    lane = lax.broadcasted_iota(jnp.int32, (tq, 128), 1)

    def rows(tile):
        return pl.ds(pl.multiple_of(tile * tq, tq), tq)

    def score_own(tile, score):
        x = kq[rows(tile), :].astype(jnp.float32)
        q = jnp.where(lane >= HEAD, pltpu.roll(x, HEAD, 1) * 0.125, 0.0).astype(jnp.bfloat16)
        qz[rows(tile), :] = q
        s = lax.dot_general(kq[rows(tile), :], q, NT, preferred_element_type=jnp.float32)
        krow = lax.broadcasted_iota(jnp.int32, (tq, tq), 0)
        qcol = lax.broadcasted_iota(jnp.int32, (tq, tq), 1)
        s = jnp.where(krow <= qcol, s, -1e30)
        score[...] = s
        newer = jnp.max(s, axis=0, keepdims=True)
        top[tile] = newer
        return newer

    def weigh_own(tile, score, newer):
        weights = jnp.exp(score[...] - newer).astype(jnp.bfloat16)
        acc[tile] = jnp.dot(vt[:, rows(tile)], weights, preferred_element_type=jnp.float32)

    def own(i, newer):
        t = 2 * i
        following = jnp.minimum(t + 1, spare)
        later = score_own(following, score1)
        weigh_own(t, score0, newer)
        after = jnp.minimum(t + 2, spare)
        newer = score_own(after, score0)
        weigh_own(following, score1, later)
        return newer

    lax.fori_loop(0, lax.div(tiles + 1, 2), own, score_own(0, score0))

    def score_pair(at, score):
        q, k = lax.div(steps[at], 256), lax.rem(steps[at], 256)
        s = lax.dot_general(kq[rows(k), :], qz[rows(q), :], NT, preferred_element_type=jnp.float32)
        score[...] = s
        old = top[q]
        newer = jnp.maximum(old, jnp.max(s, axis=0, keepdims=True))
        top[q] = newer
        return newer, jnp.exp(old - newer)

    def weigh_pair(at, score, state):
        q, k = lax.div(steps[at], 256), lax.rem(steps[at], 256)
        weights = jnp.exp(score[...] - state[0]).astype(jnp.bfloat16)
        part = jnp.dot(vt[:, rows(k)], weights, preferred_element_type=jnp.float32)
        acc[q] = acc[q] * state[1] + part

    def pair(i, state):
        t = 2 * i
        later = score_pair(t + 1, score1)
        weigh_pair(t, score0, state)
        state = score_pair(t + 2, score0)
        weigh_pair(t + 1, score1, later)
        return state

    lax.fori_loop(0, lax.div(listed + 1, 2), pair, score_pair(0, score0))

    er = lax.broadcasted_iota(jnp.int32, (BLOCK, BLOCK), 0)
    ec = lax.broadcasted_iota(jnp.int32, (BLOCK, BLOCK), 1)
    eye = jnp.where(er == ec, 1.0, 0.0).astype(jnp.bfloat16)
    low = ec < HEAD

    def put(pos):
        f = where_from[pos]
        return pltpu.make_async_copy(
            flat.at[pos], out.at[pl.ds(lax.div(f, depth) * 4, 4), lax.rem(f, depth) + offset], out_sem
        )

    def finish(tile, c):
        o = (acc[tile, 0:HEAD] / acc[tile, HEAD : HEAD + 1]).astype(jnp.bfloat16)
        for t in range(TILE):
            pos = tile * TILE + t
            piece = o[:, t * BLOCK : (t + 1) * BLOCK]
            both = jnp.concatenate([piece, piece], axis=0)
            nat = lax.dot_general(eye, both, NT, preferred_element_type=jnp.float32)
            packed = jnp.where(low[0:HEAD], nat[0:HEAD], nat[HEAD:BLOCK]).astype(jnp.bfloat16)
            flat[pos] = packed.reshape(4, 16, 128)

        for t in range(TILE):
            pos = tile * TILE + t

            @pl.when(where_from[pos] >= 0)
            def _():
                put(pos).start()

        return c

    lax.fori_loop(0, tiles, finish, 0)

    def left(i, c):
        put(0).wait()
        return c

    lax.fori_loop(0, total, left, 0)


def attend(unit, count, recv, offset, total, earlier=None):
    n, depth = recv.shape[:2]
    tiles = -(-(depth * n + depth * (TILE - 1)) // TILE)
    pairs = depth // 2 * 120 + depth % 2 * 28
    tq = TILE * BLOCK
    smem = pl.BlockSpec(memory_space=pltpu.SMEM)
    hbm = pl.BlockSpec(memory_space=pl.ANY)
    first = earlier is None
    return pl.pallas_call(
        functools.partial(attend_kernel, depth, offset, n),
        out_shape=jax.ShapeDtypeStruct((n * 4, total, 16, 128), jnp.bfloat16),
        in_specs=[smem, smem, hbm, smem if first else hbm],
        input_output_aliases={} if first else {3: 0},
        out_specs=pl.BlockSpec(memory_space=pl.ANY),
        scratch_shapes=[
            pltpu.VMEM(((tiles + 1) * tq, 128), jnp.bfloat16),
            pltpu.VMEM(((tiles + 1) * tq, 128), jnp.bfloat16),
            pltpu.VMEM((HEAD + 16, (tiles + 1) * tq), jnp.bfloat16),
            pltpu.VMEM((tq, tq), jnp.float32),
            pltpu.VMEM((tq, tq), jnp.float32),
            pltpu.VMEM((tiles + 1, 1, tq), jnp.float32),
            pltpu.VMEM((tiles + 1, HEAD + 16, tq), jnp.float32),
            pltpu.VMEM((tiles * TILE, 4, 16, 128), jnp.bfloat16),
            pltpu.SMEM((tiles * TILE + 4,), jnp.int32),
            pltpu.SMEM((pairs + 4,), jnp.int32),
            pltpu.SemaphoreType.DMA((depth, 2)),
            pltpu.SemaphoreType.DMA,
        ],
        compiler_params=pltpu.CompilerParams(vmem_limit_bytes=60 * 2**20),
        cost_estimate=pl.CostEstimate(
            flops=depth * 10**10, bytes_accessed=depth * 4 * 10**7, transcendentals=depth * 3 * 10**7
        ),
    )(unit, count, recv, unit if first else earlier)


PROJ = 8


def project_kernel(target, got, w_ref, out_ref, att):
    step = pl.program_id(0)
    lane = lax.broadcasted_iota(jnp.int32, (16, 128), 1)

    def piece(entry, z):
        owner, slot = lax.div(entry, FULL) * 4 + z, lax.rem(entry, FULL)
        return got[owner, slot].astype(jnp.float32)

    for t in range(PROJ):
        for pair in range(2):
            at = (step * PROJ + t) * 4 + pair * 2
            ea, eb = target[at], target[at + 1]
            for z in range(4):
                even, odd = piece(ea, z), piece(eb, z)
                cols = slice(z * 256 + pair * 128, z * 256 + pair * 128 + 128)
                lo = jnp.where(lane < HEAD, even, pltpu.roll(odd, HEAD, 1))
                hi = jnp.where(lane < HEAD, pltpu.roll(even, HEAD, 1), odd)
                att[t * 32 : t * 32 + 16, cols] = lo.astype(jnp.bfloat16)
                att[t * 32 + 16 : t * 32 + 32, cols] = hi.astype(jnp.bfloat16)
    mixed = jnp.zeros((PROJ * 32, 1024), jnp.float32)
    for z in range(4):
        mixed += jnp.dot(att[:, z * 256 : (z + 1) * 256], w_ref[z], preferred_element_type=jnp.float32)
    mixed = mixed.astype(jnp.bfloat16)
    for z in range(4):
        out_ref[z] = mixed[:, z * 256 : (z + 1) * 256].reshape(PROJ, 2, 16, 256)


def project(target, got, w_full, blocks):
    return pl.pallas_call(
        project_kernel,
        out_shape=jax.ShapeDtypeStruct((4, blocks, 2, 16, 256), jnp.bfloat16),
        grid_spec=pltpu.PrefetchScalarGridSpec(
            num_scalar_prefetch=1,
            grid=(blocks // PROJ,),
            in_specs=[
                pl.BlockSpec(got.shape, lambda i, *_: (0, 0, 0, 0)),
                pl.BlockSpec(w_full.shape, lambda i, *_: (0, 0, 0)),
            ],
            out_specs=pl.BlockSpec((4, PROJ, 2, 16, 256), lambda i, *_: (0, i, 0, 0, 0)),
            scratch_shapes=[pltpu.VMEM((PROJ * 32, 1024), jnp.bfloat16)],
        ),
    )(target, got, w_full)


def route(depth, *args):
    return steps(depth, *args)


def steps(depth, target, unit, count, queries, keys, values, w_out):
    n = lax.axis_size("seq")
    blocks = queries.shape[0] // BLOCK

    def exchange(x, axes):
        return lax.all_to_all(x, axes, split_axis=0, concat_axis=0, tiled=True)

    one, two = pack(target, queries, keys, values, n, depth)
    one = exchange(one, "seq")
    one, two = lax.optimization_barrier((one, two))
    two = exchange(two, "seq")
    answers = attend(unit[:FIRST], count[: FIRST * n], one, 0, depth)
    two, w_out = lax.optimization_barrier((two, w_out))
    w_full = exchange(jnp.broadcast_to(w_out[None], (4,) + w_out.shape), "head")
    answers = attend(unit[FIRST:depth], count[FIRST * n : depth * n], two, FIRST, depth, answers)
    got = exchange(answers, ("seq", "head"))
    mixed = project(target, got, w_full, blocks)
    back = exchange(mixed, "head")
    return back.transpose(1, 2, 0, 3, 4).reshape(queries.shape)


def body(queries, keys, values, cluster, w_out):
    fits, target, unit, count = tables(cluster)
    return lax.cond(
        fits,
        functools.partial(route, MAIN),
        functools.partial(route, FULL),
        target,
        unit,
        count,
        queries,
        keys,
        values,
        w_out,
    )


def solution(mesh):
    placed = (P("seq", "head"), P("seq", "head"), P("seq", "head"), P("seq", None), P("head", None))
    return jax.shard_map(
        body, mesh=mesh, in_specs=placed, out_specs=P("seq", "head"), check_vma=False
    )
```

```python
import functools

import jax
import jax.numpy as jnp
from jax import lax
from jax.experimental import pallas as pl
from jax.experimental.pallas import tpu as pltpu
from jax.sharding import PartitionSpec as P


BLOCK = 128
HEAD = 64
MAIN = 5
CUTS = (2,)
FULL = 8
TILE = 4
NT = (((1,), (1,)), ((), ()))


def tables(cluster):
    n = lax.axis_size("seq")
    me = lax.axis_index("seq")
    blocks = cluster.shape[0]
    mine = cluster.reshape(blocks)
    everyone = lax.all_to_all(
        jnp.broadcast_to(mine[None, :], (n, blocks)), "seq", split_axis=0, concat_axis=0, tiled=True
    )
    ids = jnp.arange(n, dtype=jnp.int32)
    heads = jnp.arange(4, dtype=jnp.int32)
    counts = jnp.sum((everyone[:, :, None] == ids).astype(jnp.int32), axis=1)
    weight = jnp.max(counts, axis=0)
    before = ids[None, :] < ids[:, None]
    rank2 = jnp.sum((before & (weight == 2)[None, :]).astype(jnp.int32), axis=1)
    rank1 = jnp.sum((before & (weight == 1)[None, :]).astype(jnp.int32), axis=1)
    twos = 4 * jnp.sum((weight == 2).astype(jnp.int32))
    full, rem = twos // n, twos % n
    light = n - rem
    heavy = jnp.maximum(rem, 1)
    k2 = rank2[:, None] * 4 + heads
    k = rank1[:, None] * 4 + heads
    a = jnp.maximum(MAIN - 2 * full, 0) * light
    b = jnp.maximum(MAIN - 2 - 2 * full, 0) * rem
    c0 = jnp.maximum(MAIN, 2 * full)
    c = (FULL - c0) * light
    kb, kc = k - a, k - a - b
    kd = kc - c
    owner1 = jnp.where(
        k < a, rem + k % light, jnp.where(kb < b, kb % heavy, jnp.where(kc < c, rem + kc % light, kd % heavy))
    )
    slot1 = jnp.where(
        k < a,
        2 * full + k // light,
        jnp.where(
            kb < b,
            2 * full + 2 + kb // heavy,
            jnp.where(kc < c, c0 + kc // light, jnp.maximum(MAIN, 2 * full + 2) + kd // heavy),
        ),
    )
    two = (weight == 2)[:, None]
    used = (weight > 0)[:, None]
    owner = jnp.where(two, k2 % n, owner1)
    slot = jnp.where(two, 2 * (k2 // n), slot1)
    fits = jnp.all(~used | (slot + weight[:, None] <= MAIN))
    hit = mine[:, None] == ids[None, :]
    earlier = jnp.arange(blocks)[None, :] < jnp.arange(blocks)[:, None]
    second = jnp.sum((earlier & (mine[None, :] == mine[:, None])).astype(jnp.int32), axis=1)
    target = jnp.sum(jnp.where(hit[:, :, None], (owner * FULL + slot)[None], 0), axis=1) + second[:, None]
    slots = jnp.arange(FULL, dtype=jnp.int32)
    held = (used & (owner == me))[None] & (slot[None] == slots[:, None, None])
    unit = jnp.sum(jnp.where(held, weight[None, :, None], 0), axis=(1, 2))
    count = jnp.sum(jnp.where(jnp.any(held, axis=2)[:, None, :], counts[None], 0), axis=2)
    return fits, target.reshape(blocks * 4), unit, count.reshape(FULL * n)


PACK = 4


def pack_kernel(target, q_ref, k_ref, v_ref, one_ref, two_ref, stage, eye, sems):
    step = pl.program_id(0)
    par = lax.rem(step, 2)

    @pl.when(step == 0)
    def _():
        r = lax.broadcasted_iota(jnp.int32, (256, 256), 0)
        c = lax.broadcasted_iota(jnp.int32, (256, 256), 1)
        eye[...] = jnp.where(r == c, 1.0, 0.0).astype(jnp.bfloat16)

    def send(p, i):
        t = target[step * (PACK * 4) + i]
        owner, slot = lax.div(t, FULL), lax.rem(t, FULL)

        for ref, low, high in zip((one_ref, two_ref), (0,) + CUTS, CUTS + (FULL,)):

            @pl.when((slot >= low) & (slot < high))
            def _():
                pltpu.make_async_copy(stage.at[p, i], ref.at[owner, slot - low], sems.at[p, i]).start()

    def wait(p, i):
        pltpu.make_async_copy(stage.at[p, i], one_ref.at[0, 0], sems.at[p, i]).wait()

    @pl.when(step >= 2)
    def _():
        for i in range(PACK * 4):
            wait(par, i)

    lane = lax.broadcasted_iota(jnp.int32, (BLOCK, 128), 1)
    for t in range(PACK):
        rows = slice(t * BLOCK, (t + 1) * BLOCK)
        vt = lax.dot_general(eye[...], v_ref[rows, :], NT, preferred_element_type=jnp.float32)
        vt = vt.astype(jnp.bfloat16)
        for pair in range(2):
            cols = slice(pair * 128, (pair + 1) * 128)
            q = q_ref[rows, cols].astype(jnp.float32)
            k = k_ref[rows, cols].astype(jnp.float32)
            even = jnp.where(lane < HEAD, q, pltpu.roll(k, HEAD, 1))
            odd = jnp.where(lane < HEAD, pltpu.roll(q, HEAD, 1), k)
            stage[par, t * 4 + pair * 2, 0:BLOCK, :] = even.astype(jnp.bfloat16)
            stage[par, t * 4 + pair * 2 + 1, 0:BLOCK, :] = odd.astype(jnp.bfloat16)
        for h in range(4):
            stage[par, t * 4 + h, BLOCK : BLOCK + HEAD, :] = vt[h * HEAD : (h + 1) * HEAD]
    for i in range(PACK * 4):
        send(par, i)

    @pl.when(step == pl.num_programs(0) - 1)
    def _():
        for i in range(PACK * 4):
            wait(1 - par, i)
        for i in range(PACK * 4):
            wait(par, i)


def pack(target, queries, keys, values, n, depth):
    rows, width = queries.shape
    tile = pl.BlockSpec((PACK * BLOCK, width), lambda i, *_: (i, 0))
    return pl.pallas_call(
        pack_kernel,
        out_shape=[
            jax.ShapeDtypeStruct((n, high - low, BLOCK + HEAD, 128), jnp.bfloat16)
            for low, high in zip((0,) + CUTS, CUTS + (depth,))
        ],
        grid_spec=pltpu.PrefetchScalarGridSpec(
            num_scalar_prefetch=1,
            grid=(rows // (PACK * BLOCK),),
            in_specs=[tile, tile, tile],
            out_specs=[pl.BlockSpec(memory_space=pl.ANY)] * 2,
            scratch_shapes=[
                pltpu.VMEM((2, PACK * 4, BLOCK + HEAD, 128), jnp.bfloat16),
                pltpu.VMEM((256, 256), jnp.bfloat16),
                pltpu.SemaphoreType.DMA((2, PACK * 4)),
            ],
        ),
    )(target, queries, keys, values)


def attend_kernel(
    depth, offset, n, unit, count, recv, _, out, kq, qz, vt, score0, score1, top, acc, flat, where_from, steps, in_sems, out_sem
):
    tq = TILE * BLOCK
    spare = acc.shape[0] - 1

    def fetch(pos, s, j, u):
        at = pl.multiple_of(pos * BLOCK, BLOCK)
        return (
            pltpu.make_async_copy(
                recv.at[s, j, pl.ds(0, BLOCK), :], kq.at[pl.ds(at, BLOCK), :], in_sems.at[u, 0]
            ),
            pltpu.make_async_copy(
                recv.at[s, j, pl.ds(BLOCK, HEAD), :],
                vt.at[pl.ds(0, HEAD), pl.ds(at, BLOCK)],
                in_sems.at[u, 1],
            ),
        )

    def fetch_unit(u, carry):
        base, listed, total = carry
        w = unit[u]

        def source(s, pos):
            here = jnp.where(w > 0, count[u * n + s], 0)
            for r in range(2):

                @pl.when(here > r)
                def _():
                    where_from[pos + r] = s * depth + u + r
                    for c in fetch(pos + r, s, u + r, u):
                        c.start()

            return pos + here

        end = lax.fori_loop(0, n, source, base)
        stop = lax.div(end + TILE - 1, TILE) * TILE

        def blank(pos, c):
            at = pl.multiple_of(pos * BLOCK, BLOCK)
            vt[0:HEAD, pl.ds(at, BLOCK)] = jnp.zeros((HEAD, BLOCK), jnp.bfloat16)
            where_from[pos] = -1
            return c

        lax.fori_loop(end, stop, blank, 0)
        first, last = lax.div(base, TILE), lax.div(stop, TILE)

        def list_tile(q, at):
            def one(k, at):
                steps[at] = q * 256 + k
                return at + 1

            return lax.fori_loop(first, q, one, at)

        return stop, lax.fori_loop(first, last, list_tile, listed), total + end - base

    stop, listed, total = lax.fori_loop(0, depth, fetch_unit, (0, 0, 0))
    tiles = lax.div(stop, TILE)
    for extra in range(TILE):
        where_from[stop + extra] = -1
    for extra in range(3):
        steps[listed + extra] = spare * 256 + spare
    ones = lax.broadcasted_iota(jnp.int32, (16, vt.shape[1]), 0)
    vt[HEAD : HEAD + 16, :] = jnp.where(ones == 0, 1.0, 0.0).astype(jnp.bfloat16)

    def arrive(u, c):
        def one(s, c):
            here = jnp.where(unit[u] > 0, count[u * n + s], 0)
            for r in range(2):

                @pl.when(here > r)
                def _():
                    for cp in fetch(0, 0, 0, u):
                        cp.wait()

            return c

        return lax.fori_loop(0, n, one, c)

    lax.fori_loop(0, depth, arrive, 0)

    lane = lax.broadcasted_iota(jnp.int32, (tq, 128), 1)

    def rows(tile):
        return pl.ds(pl.multiple_of(tile * tq, tq), tq)

    def score_own(tile, score):
        x = kq[rows(tile), :].astype(jnp.float32)
        q = jnp.where(lane >= HEAD, pltpu.roll(x, HEAD, 1) * 0.125, 0.0).astype(jnp.bfloat16)
        qz[rows(tile), :] = q
        s = lax.dot_general(kq[rows(tile), :], q, NT, preferred_element_type=jnp.float32)
        krow = lax.broadcasted_iota(jnp.int32, (tq, tq), 0)
        qcol = lax.broadcasted_iota(jnp.int32, (tq, tq), 1)
        s = jnp.where(krow <= qcol, s, -1e30)
        score[...] = s
        newer = jnp.max(s, axis=0, keepdims=True)
        top[tile] = newer
        return newer

    def weigh_own(tile, score, newer):
        weights = jnp.exp(score[...] - newer).astype(jnp.bfloat16)
        acc[tile] = jnp.dot(vt[:, rows(tile)], weights, preferred_element_type=jnp.float32)

    def own(i, newer):
        t = 2 * i
        following = jnp.minimum(t + 1, spare)
        later = score_own(following, score1)
        weigh_own(t, score0, newer)
        after = jnp.minimum(t + 2, spare)
        newer = score_own(after, score0)
        weigh_own(following, score1, later)
        return newer

    lax.fori_loop(0, lax.div(tiles + 1, 2), own, score_own(0, score0))

    def score_pair(at, score):
        q, k = lax.div(steps[at], 256), lax.rem(steps[at], 256)
        s = lax.dot_general(kq[rows(k), :], qz[rows(q), :], NT, preferred_element_type=jnp.float32)
        score[...] = s
        old = top[q]
        newer = jnp.maximum(old, jnp.max(s, axis=0, keepdims=True))
        top[q] = newer
        return newer, jnp.exp(old - newer)

    def weigh_pair(at, score, state):
        q, k = lax.div(steps[at], 256), lax.rem(steps[at], 256)
        weights = jnp.exp(score[...] - state[0]).astype(jnp.bfloat16)
        part = jnp.dot(vt[:, rows(k)], weights, preferred_element_type=jnp.float32)
        acc[q] = acc[q] * state[1] + part

    def pair(i, state):
        t = 2 * i
        later = score_pair(t + 1, score1)
        weigh_pair(t, score0, state)
        state = score_pair(t + 2, score0)
        weigh_pair(t + 1, score1, later)
        return state

    lax.fori_loop(0, lax.div(listed + 1, 2), pair, score_pair(0, score0))

    er = lax.broadcasted_iota(jnp.int32, (BLOCK, BLOCK), 0)
    ec = lax.broadcasted_iota(jnp.int32, (BLOCK, BLOCK), 1)
    eye = jnp.where(er == ec, 1.0, 0.0).astype(jnp.bfloat16)
    low = ec < HEAD

    def put(pos):
        f = where_from[pos]
        return pltpu.make_async_copy(
            flat.at[pos], out.at[pl.ds(lax.div(f, depth) * 4, 4), lax.rem(f, depth) + offset], out_sem
        )

    def finish(tile):
        o = (acc[tile, 0:HEAD] / acc[tile, HEAD : HEAD + 1]).astype(jnp.bfloat16)
        for t in range(TILE):
            pos = tile * TILE + t
            piece = o[:, t * BLOCK : (t + 1) * BLOCK]
            both = jnp.concatenate([piece, piece], axis=0)
            nat = lax.dot_general(eye, both, NT, preferred_element_type=jnp.float32)
            packed = jnp.where(low[0:HEAD], nat[0:HEAD], nat[HEAD:BLOCK]).astype(jnp.bfloat16)
            flat[pos] = packed.reshape(4, 16, 128)

    def finish_two(i, c):
        finish(2 * i)
        finish(2 * i + 1)
        for t in range(2 * TILE):
            pos = i * 2 * TILE + t

            @pl.when(where_from[pos] >= 0)
            def _():
                put(pos).start()

        return c

    lax.fori_loop(0, lax.div(tiles + 1, 2), finish_two, 0)

    def left(i, c):
        put(0).wait()
        return c

    lax.fori_loop(0, total, left, 0)


def attend(unit, count, recv, offset, total, earlier=None):
    n, depth = recv.shape[:2]
    tiles = -(-(depth * n + depth * (TILE - 1)) // TILE)
    pairs = depth // 2 * 120 + depth % 2 * 28
    tq = TILE * BLOCK
    smem = pl.BlockSpec(memory_space=pltpu.SMEM)
    hbm = pl.BlockSpec(memory_space=pl.ANY)
    first = earlier is None
    return pl.pallas_call(
        functools.partial(attend_kernel, depth, offset, n),
        out_shape=jax.ShapeDtypeStruct((n * 4, total, 16, 128), jnp.bfloat16),
        in_specs=[smem, smem, hbm, smem if first else hbm],
        input_output_aliases={} if first else {3: 0},
        out_specs=pl.BlockSpec(memory_space=pl.ANY),
        scratch_shapes=[
            pltpu.VMEM(((tiles + 1) * tq, 128), jnp.bfloat16),
            pltpu.VMEM(((tiles + 1) * tq, 128), jnp.bfloat16),
            pltpu.VMEM((HEAD + 16, (tiles + 1) * tq), jnp.bfloat16),
            pltpu.VMEM((tq, tq), jnp.float32),
            pltpu.VMEM((tq, tq), jnp.float32),
            pltpu.VMEM((tiles + 1, 1, tq), jnp.float32),
            pltpu.VMEM((tiles + 1, HEAD + 16, tq), jnp.float32),
            pltpu.VMEM(((tiles + 1) * TILE, 4, 16, 128), jnp.bfloat16),
            pltpu.SMEM(((tiles + 1) * TILE,), jnp.int32),
            pltpu.SMEM((pairs + 4,), jnp.int32),
            pltpu.SemaphoreType.DMA((depth, 2)),
            pltpu.SemaphoreType.DMA,
        ],
        compiler_params=pltpu.CompilerParams(vmem_limit_bytes=60 * 2**20),
        cost_estimate=pl.CostEstimate(
            flops=depth * 10**10, bytes_accessed=depth * 4 * 10**7, transcendentals=depth * 3 * 10**7
        ),
    )(unit, count, recv, unit if first else earlier)


PROJ = 8


def project_kernel(target, group, got, w0, w1, w2, w3, out_ref, att):
    step = pl.program_id(0)
    lane = lax.broadcasted_iota(jnp.int32, (16, 128), 1)

    def piece(entry, z):
        owner, slot = lax.div(entry, FULL) * 4 + z, lax.rem(entry, FULL)
        return got[owner, slot].astype(jnp.float32)

    for t in range(PROJ):
        for pair in range(2):
            at = (step * PROJ + t) * 4 + pair * 2
            ea, eb = target[at], target[at + 1]
            for z in range(4):
                source = lax.rem(group[0] + z, 4)
                even, odd = piece(ea, source), piece(eb, source)
                cols = slice(z * 256 + pair * 128, z * 256 + pair * 128 + 128)
                lo = jnp.where(lane < HEAD, even, pltpu.roll(odd, HEAD, 1))
                hi = jnp.where(lane < HEAD, pltpu.roll(even, HEAD, 1), odd)
                att[t * 32 : t * 32 + 16, cols] = lo.astype(jnp.bfloat16)
                att[t * 32 + 16 : t * 32 + 32, cols] = hi.astype(jnp.bfloat16)
    mixed = jnp.zeros((PROJ * 32, 1024), jnp.float32)
    for z, w in enumerate((w0, w1, w2, w3)):
        mixed += jnp.dot(att[:, z * 256 : (z + 1) * 256], w[...], preferred_element_type=jnp.float32)
    mixed = mixed.astype(jnp.bfloat16)
    for z in range(4):
        out_ref[z] = mixed[:, z * 256 : (z + 1) * 256].reshape(PROJ, 2, 16, 256)


def project(target, got, weights, blocks):
    group = lax.axis_index("head").reshape(1)
    return pl.pallas_call(
        project_kernel,
        out_shape=jax.ShapeDtypeStruct((4, blocks, 2, 16, 256), jnp.bfloat16),
        grid_spec=pltpu.PrefetchScalarGridSpec(
            num_scalar_prefetch=2,
            grid=(blocks // PROJ,),
            in_specs=[
                pl.BlockSpec(got.shape, lambda i, *_: (0, 0, 0, 0)),
            ]
            + [pl.BlockSpec(w.shape, lambda i, *_: (0, 0)) for w in weights],
            out_specs=pl.BlockSpec((4, PROJ, 2, 16, 256), lambda i, *_: (0, i, 0, 0, 0)),
            scratch_shapes=[pltpu.VMEM((PROJ * 32, 1024), jnp.bfloat16)],
        ),
    )(target, group, got, *weights)


def route(depth, *args):
    return steps(depth, *args)


def steps(depth, target, unit, count, queries, keys, values, w_out):
    n = lax.axis_size("seq")
    blocks = queries.shape[0] // BLOCK

    def exchange(x, axes):
        return lax.all_to_all(x, axes, split_axis=0, concat_axis=0, tiled=True)

    one, two = pack(target, queries, keys, values, n, depth)
    one = exchange(one, "seq")
    one, two = lax.optimization_barrier((one, two))
    two = exchange(two, "seq")
    weights = [w_out]
    for r in (1, 2, 3):
        weights.append(lax.ppermute(w_out, "head", [((z + r) % 4, z) for z in range(4)]))
    a = CUTS[0]
    answers = attend(unit[:a], count[: a * n], one, 0, depth)
    answers = attend(unit[a:depth], count[a * n : depth * n], two, a, depth, answers)
    got = exchange(answers, ("seq", "head"))
    mixed = project(target, got, weights, blocks)
    back = exchange(mixed, "head")
    return back.transpose(1, 2, 0, 3, 4).reshape(queries.shape)


def body(queries, keys, values, cluster, w_out):
    fits, target, unit, count = tables(cluster)
    return lax.cond(
        fits,
        functools.partial(route, MAIN),
        functools.partial(route, FULL),
        target,
        unit,
        count,
        queries,
        keys,
        values,
        w_out,
    )


def solution(mesh):
    placed = (P("seq", "head"), P("seq", "head"), P("seq", "head"), P("seq", None), P("head", None))
    return jax.shard_map(
        body, mesh=mesh, in_specs=placed, out_specs=P("seq", "head"), check_vma=False
    )
```
